32 devices in a mesh: sec: 2 (over x), tile: 16 (over z, y, core).
Axes of the slice: x: 2, y: 2, z: 4, core: 2. Of those that a mesh axis runs over, the one named last changes fastest.
Arguments:
- start_modes: bfloat16 [16, 24, 384, 384], P('sec', None, 'tile'), may hold values from -6 to 6
- permittivity: bfloat16 [16, 384, 384], P('sec', 'tile'), may hold values from 1 to 12
- heights: int32 [16], replicated, may hold values from 192 to 384, as said below
Outputs:
- mode_fields: bfloat16 [16, 24, 384, 384], P('sec', None, 'tile')
- coupling: float32 [16, 24, 24], P('sec')
The draws below stay inside these ranges and needn't reach their ends.
Inputs may be any that keep to these rules, and one draw needn't show every extreme that they name: heights[s] is the number of rows in use of section s, counted from row 0; some section uses all 384 rows.
All inputs are finite; a program needn't handle non-finite values.
Results may differ from the reference program's by a relative error of at most 0.001.
Values may be sent and summed in bfloat16 or wider, within the bound.
A program may use at most 128 MiB of HBM per device.

```python
import math
import jax
import jax.numpy as jnp
from jax import lax

M = 24
GC = 384
GR = 384
STEPS = 3
DEG = 4
SECTIONS = 16


def draw_heights(key, part):
    first, second = jax.random.split(jax.random.fold_in(key, 11))
    drawn = jax.random.randint(first, (SECTIONS,), GR // 2, GR + 1)
    chosen = jax.random.randint(second, (), 0, SECTIONS)
    return jnp.where(jnp.arange(SECTIONS) == chosen, GR, drawn).astype(jnp.int32)


def block_scale(stream_key, shape, pieces, least, largest):
    factor_of, own = 1.0, jax.random.fold_in(stream_key, 6)
    for position, shards_of in pieces:
        steps = jnp.exp(jax.random.uniform(jax.random.fold_in(own, position), (shards_of,), jnp.float32, least / len(pieces), largest / len(pieces)))
        factor_of = factor_of * jnp.repeat(steps, shape[position] // shards_of).reshape([-1 if axis == position else 1 for axis in range(len(shape))])
    return factor_of


def scatter_about(key, extent, width, most, cuts=(), kind=jnp.bfloat16):
    level = block_scale(key, extent, cuts, -0.22, 0.18) if cuts else 1.0
    values = jax.random.normal(key, extent, jnp.float32) * width * level
    return jnp.minimum(jnp.maximum(values, -most), most).astype(kind)


def setup_inputs(seed: int = 0) -> dict:
    seeds = jax.random.split(jax.random.key(seed), 4)
    start_modes = scatter_about(seeds[0], (SECTIONS, M, GR, GC), 1.0, 6.0, ((0, 2), (2, 16)))
    permittivity = jnp.clip(jnp.exp(math.log(12.0) - 2.4849066 * jax.random.uniform(seeds[1], (SECTIONS, GR, GC), jnp.float32) ** block_scale(seeds[1], (SECTIONS, GR, GC), ((0, 2), (1, 16)), -0.2, 0.2)), 1.0, 12.0).astype(jnp.bfloat16)
    heights = draw_heights(jax.random.fold_in(seeds[3], 71), 0)
    return {"start_modes": start_modes, "permittivity": permittivity, "heights": heights}


SHIFT_DIAG = 3.0
EPS_WEIGHT = 0.25
LOWER_EDGE = 2.0
UPPER_EDGE = 10.75

def chebyshev_terms(degree):
    center = 0.5 * (UPPER_EDGE + LOWER_EDGE)
    radius = 0.5 * (UPPER_EDGE - LOWER_EDGE)
    anchor = -center / radius
    values = [1.0, anchor]
    for order in range(1, degree):
        values.append(2.0 * anchor * values[order] - values[order - 1])
    return (center, radius, values)

def scaled_apply(padded, field, diag_scaled, row_mask, inverse):
    sided = jnp.pad(field, ((0, 0), (0, 0), (0, 0), (1, 1)))
    beside = padded[:, :, 2:, :] + padded[:, :, :-2, :] + sided[:, :, :, 2:] + sided[:, :, :, :-2]
    return (diag_scaled * field - inverse * beside) * row_mask

def filter_steps(field, apply_once, degree):
    center, radius, values = chebyshev_terms(degree)
    previous = field
    current = apply_once(field) * (1.0 / values[1])
    for order in range(1, degree):
        upcoming = apply_once(current) * (2.0 * values[order] / values[order + 1]) - previous * (values[order - 1] / values[order + 1])
        previous = current
        current = upcoming
    return current

def orthonormal(field):
    gram = jnp.einsum('smrc,snrc->smn', field, field, precision=lax.Precision.HIGHEST)
    lower = jnp.linalg.cholesky(gram)
    flat = field.reshape(field.shape[0], field.shape[1], -1)
    solved = lax.linalg.triangular_solve(lower, flat, left_side=True, lower=True)
    return solved.reshape(field.shape)

def reference(start_modes, permittivity, heights):
    center, radius, values = chebyshev_terms(DEG)
    inverse = 1.0 / radius
    row_ids = jnp.arange(GR, dtype=jnp.int32)

    def one_section(packed):
        start, perm, height = packed
        row_mask = (row_ids < height).astype(jnp.float32)[None, None, :, None]
        diag_scaled = ((4.0 + SHIFT_DIAG - EPS_WEIGHT * perm.astype(jnp.float32) - center) * inverse)[None, None]

        def apply_once(current):
            padded = jnp.pad(current, ((0, 0), (0, 0), (1, 1), (0, 0)))
            return scaled_apply(padded, current, diag_scaled, row_mask, inverse)
        field = start.astype(jnp.float32)[None] * row_mask
        for step in range(STEPS):
            field = orthonormal(filter_steps(field, apply_once, DEG))
        return (field[0] * GC).astype(jnp.bfloat16)
    mode_fields = lax.map(one_section, (start_modes, permittivity, heights))
    following = jnp.concatenate([mode_fields[1:], jnp.zeros_like(mode_fields[:1])], 0)

    def pair(packed):
        here, there = packed
        return jnp.dot(here.reshape(M, -1).astype(jnp.float32), there.reshape(M, -1).T.astype(jnp.float32), preferred_element_type=jnp.float32)
    coupling = lax.map(pair, (mode_fields, following)) / (GC * math.sqrt(GC))
    return (mode_fields, coupling)
```

```python
import functools
import math

import jax
import jax.numpy as jnp
from jax import lax
from jax.experimental import pallas as pl
from jax.experimental.pallas import tpu as pltpu
from jax.sharding import PartitionSpec as P

STEPS = 3
DEG = 4
SHIFT_DIAG = 3.0
EPS_WEIGHT = 0.25
LOWER_EDGE = 2.0
UPPER_EDGE = 10.75
CENTER = 0.5 * (UPPER_EDGE + LOWER_EDGE)
RADIUS = 0.5 * (UPPER_EDGE - LOWER_EDGE)
WIDTH = STEPS * DEG
LANES = 128
SLOT = 32
CHUNKS = 1
PER = LANES // SLOT

ROOTS = [CENTER + RADIUS * math.cos(math.pi * (2 * k + 1) / (2 * DEG)) for k in (0, 3, 1, 2)]

NT = (((1,), (1,)), ((), ()))
MESH = pl.DeviceIdType.MESH
F32, BF16 = jnp.float32, jnp.bfloat16


def iota(shape, dim):
    return lax.broadcasted_iota(jnp.int32, shape, dim)


def dot32(a, b):
    return jnp.dot(a, b, preferred_element_type=F32)


def dot_nt(a, b):
    return lax.dot_general(a, b, NT, preferred_element_type=F32)


def interleave(columns, groups, inverse=False):
    row, col = iota((columns, columns), 0), iota((columns, columns), 1)
    if inverse:
        row, col = col, row
    return (row == groups * (col % LANES) + col // LANES).astype(BF16)


def inner_size(tiles):
    return max(n for n in range(1, tiles + 1) if tiles % n == 0 and n * n <= tiles)


def split_bf16(value):
    high = value.astype(BF16).astype(F32)
    return high, value - high


def hops_of(strip):
    plan, done = [], 0
    while done < WIDTH:
        rows = min(strip, WIDTH - done)
        plan.append((len(plan) + 1, rows, done))
        done += rows
    return plan


def fused_kernel(
    kept_rows,
    x_hbm,
    perm_ref,
    out_hbm,
    coup_ref,
    x_buf,
    x_own,
    x_above,
    x_below,
    p_own,
    p_above,
    p_below,
    a_ref,
    b_ref,
    q_ref,
    mix_ref,
    unmix_ref,
    split_ref,
    both_ref,
    next_ref,
    stack_ref,
    rows_ref,
    out_buf,
    wide_ref,
    pack_ref,
    near_ref,
    far_ref,
    mid_ref,
    inv_ref,
    in_sem,
    out_sem,
    halo_send,
    halo_recv,
    perm_send,
    perm_recv,
    near_send,
    near_recv,
    far_send,
    far_recv,
    next_send,
    next_recv,
):
    sections, modes, strip, columns = x_buf.shape
    groups = columns // LANES
    packs = pack_ref.shape[0] // 2
    used = strip + 2 * WIDTH
    tiles, blocks = lax.axis_size("tile"), lax.axis_size("sec")
    me, my_sec = lax.axis_index("tile"), lax.axis_index("sec")
    near = near_ref.shape[1]
    far = far_ref.shape[1]
    pos, ring = lax.rem(me, near), me // near
    plan = hops_of(strip)
    mode_tiles = modes // 8

    barrier = pltpu.get_barrier_semaphore()

    def greet(d, carry):
        pl.semaphore_signal(barrier, inc=1, device_id={"tile": lax.rem(me + d, tiles)}, device_id_type=MESH)
        return carry

    lax.fori_loop(1, tiles, greet, 0)
    if blocks > 1:
        pl.semaphore_signal(barrier, inc=1, device_id={"sec": lax.rem(my_sec + 1, blocks)}, device_id_type=MESH)
        pl.semaphore_signal(barrier, inc=1, device_id={"sec": lax.rem(my_sec + blocks - 1, blocks)}, device_id_type=MESH)

    def load_copy(s):
        return pltpu.make_async_copy(x_hbm.at[s], x_buf.at[s], in_sem.at[s])

    def store_copy(s):
        return pltpu.make_async_copy(out_buf.at[s], out_hbm.at[s], out_sem.at[s])

    lax.fori_loop(0, sections, lambda s, c: (load_copy(s).start(), c)[1], 0)

    mix_ref[...] = interleave(columns, groups)
    unmix_ref[...] = interleave(columns, groups, True)
    wide_ref[...] = jnp.zeros_like(wide_ref)
    pack_ref[...] = jnp.zeros_like(pack_ref)

    def blank(ref, unit, lead):
        for hop, rows, done in plan:
            above, below = (WIDTH - done - rows) * unit, done * unit
            zeros = jnp.zeros((rows * unit, columns), BF16)

            @pl.when(me < hop)
            def _():
                ref[0][lead + (slice(above, above + rows * unit),)] = zeros

            @pl.when(me + hop >= tiles)
            def _():
                ref[1][lead + (slice(below, below + rows * unit),)] = zeros

    def halo_copies(own, above, below, send, recv, unit, hop, rows, done, slot, lead):
        h = hop - 1
        down = pltpu.make_async_remote_copy(
            src_ref=own.at[lead + (pl.ds((strip - rows) * unit, rows * unit),)],
            dst_ref=above.at[lead + (pl.ds((WIDTH - done - rows) * unit, rows * unit),)],
            send_sem=send.at[(0, h) + slot],
            recv_sem=recv.at[(0, h) + slot],
            device_id={"tile": lax.rem(me + hop, tiles)},
            device_id_type=MESH,
        )
        up = pltpu.make_async_remote_copy(
            src_ref=own.at[lead + (pl.ds(0, rows * unit),)],
            dst_ref=below.at[lead + (pl.ds(done * unit, rows * unit),)],
            send_sem=send.at[(1, h) + slot],
            recv_sem=recv.at[(1, h) + slot],
            device_id={"tile": lax.rem(me + tiles - hop, tiles)},
            device_id_type=MESH,
        )
        return down, up

    def x_copies(s, hop, rows, done):
        return halo_copies(x_own, x_above, x_below, halo_send, halo_recv, modes, hop, rows, done, (s,), (s,))

    def p_copies(hop, rows, done):
        return halo_copies(p_own, p_above, p_below, perm_send, perm_recv, sections, hop, rows, done, (), ())

    def each_halo(copies, action):
        for hop, rows, done in plan:
            down, up = copies(hop, rows, done)
            if action == "send":
                pl.when(me + hop < tiles)(lambda down=down: down.start())
                pl.when(me >= hop)(lambda up=up: up.start())
            elif action == "recv":
                pl.when(me >= hop)(lambda down=down: down.wait_recv())
                pl.when(me + hop < tiles)(lambda up=up: up.wait_recv())
            else:
                pl.when(me + hop < tiles)(lambda down=down: down.wait_send())
                pl.when(me >= hop)(lambda up=up: up.wait_send())

    def prepare(s):
        load_copy(s).wait()
        for m in range(modes):
            for j in range(groups):
                a_ref[j, pl.ds(m, strip, stride=modes), :] = x_buf[s, m, :, j * LANES : (j + 1) * LANES].astype(F32)
        take = max(n for n in range(1, 9) if strip % n == 0) * modes
        for r0 in range(0, strip * modes, take):
            plain = jnp.concatenate(
                [
                    jnp.concatenate([a_ref[j, r0 + r : r0 + r + modes, :] for j in range(groups)], axis=1)
                    * kept_rows[s * used + WIDTH + (r0 + r) // modes]
                    for r in range(0, take, modes)
                ],
                axis=0,
            )
            x_own[s, r0 : r0 + take, :] = dot32(plain.astype(BF16), mix_ref[...]).astype(BF16)

    perm = dot32(perm_ref[...].astype(F32).reshape(sections * strip, columns).astype(BF16), mix_ref[...])
    for s in range(sections):
        for j in range(groups):
            b_ref[j, pl.ds(s, strip, stride=sections), :] = perm[s * strip : (s + 1) * strip, j * LANES : (j + 1) * LANES]
    for j in range(groups):
        p_own[:, j * LANES : (j + 1) * LANES] = b_ref[j, 0 : strip * sections, :].astype(BF16)
    prepare(0)
    pl.semaphore_wait(barrier, tiles - 1 + (2 if blocks > 1 else 0))
    each_halo(p_copies, "send")
    each_halo(functools.partial(x_copies, 0), "send")
    blank((p_above, p_below), sections, ())
    blank((x_above, x_below), modes, (0,))

    def prepare_rest(s, carry):
        prepare(s)
        pl.when(s < 2)(lambda: each_halo(functools.partial(x_copies, s), "send"))
        blank((x_above, x_below), modes, (s,))
        return carry

    lax.fori_loop(1, sections, prepare_rest, 0)

    each_halo(p_copies, "recv")
    base = 4.0 + SHIFT_DIAG
    for part, first, rows in ((p_above, 0, WIDTH), (p_own, WIDTH, strip), (p_below, WIDTH + strip, WIDTH)):
        for j in range(groups):
            diag = base - EPS_WEIGHT * part[:, j * LANES : (j + 1) * LANES].astype(F32)
            for i, root in enumerate(ROOTS):
                q_ref[i, j, first * sections : (first + rows) * sections, :] = diag - root

    lane = iota((8, LANES), 1)
    is_first, is_last = lane == 0, lane == LANES - 1

    def tile_at(row, t):
        return pl.ds(pl.multiple_of(row * modes + t * 8, 8), 8)

    def row_of(ref, row):
        return [[ref[j, tile_at(row, t), :] for j in range(groups)] for t in range(mode_tiles)]

    def stage(src, dst, which, order, s):
        count = -(-(used - 2 * order) // CHUNKS)
        low = min(order, used - CHUNKS * count)

        def body(block, carry):
            row0 = low + block * count
            before, here = row_of(src, row0 - 1), row_of(src, row0)
            for i in range(count):
                row = row0 + i
                after = row_of(src, row + 1)
                weight = kept_rows[s * used + row]
                q = [jnp.broadcast_to(q_ref[which, j, pl.ds(row * sections + s, 1), :], (8, LANES)) for j in range(groups)]
                for t in range(mode_tiles):
                    h = here[t]
                    left = jnp.where(is_first, 0.0, pltpu.roll(h[groups - 1], 1, 1))
                    right = jnp.where(is_last, 0.0, pltpu.roll(h[0], LANES - 1, 1))
                    for j in range(groups):
                        side = (h[j - 1] if j else left) + (h[j + 1] if j < groups - 1 else right)
                        beside = (before[t][j] + after[t][j]) + side
                        dst[j, tile_at(row, t), :] = q[j] * h[j] - weight * beside
                before, here = here, after
            return carry

        if CHUNKS == 1:
            body(0, 0)
        else:
            lax.fori_loop(0, CHUNKS, body, 0)

    def place(small, target, s):
        wide_ref[:, 0:modes] = small
        moved = pltpu.roll(wide_ref[...], SLOT * lax.rem(s, PER), 1)
        pack_ref[target] = pack_ref[target] + moved

    def near_copy(i, d, slot):
        return pltpu.make_async_remote_copy(
            src_ref=pack_ref.at[i],
            dst_ref=near_ref.at[i, slot],
            send_sem=near_send.at[i, d],
            recv_sem=near_recv.at[i, slot],
            device_id={"tile": ring * near + lax.rem(pos + d, near)},
            device_id_type=MESH,
        )

    def far_copy(i, d, slot):
        return pltpu.make_async_remote_copy(
            src_ref=mid_ref.at[i],
            dst_ref=far_ref.at[i, slot],
            send_sem=far_send.at[i, d],
            recv_sem=far_recv.at[i, slot],
            device_id={"tile": lax.rem(ring + d, far) * near + pos},
            device_id_type=MESH,
        )

    def begin(i):
        for d in range(1, near):
            near_copy(i, d, pos).start()
        near_ref[i, pos] = pack_ref[i]

    def middle(i):
        for d in range(1, near):
            near_copy(i, d, lax.rem(pos + near - d, near)).wait_recv()
        total = near_ref[i, 0]
        for n in range(1, near):
            total = total + near_ref[i, n]
        mid_ref[i] = total
        for d in range(1, far):
            far_copy(i, d, ring).start()
        far_ref[i, ring] = total

    def finish(i):
        for d in range(1, far):
            far_copy(i, d, lax.rem(ring + far - d, far)).wait_recv()
        total = far_ref[i, 0]
        for n in range(1, far):
            total = total + far_ref[i, n]
        return total

    def members(i):
        return range(i * PER, min(sections, (i + 1) * PER))

    def spread(total, count):
        return [pltpu.roll(total, (LANES - SLOT * n) % LANES, 1) if n else total for n in range(count)]

    def factor(i):
        parts = spread(finish(i), len(members(i)))
        shape = (len(parts), modes, LANES)
        row, col = iota(shape, 1), iota(shape, 2)
        work = jnp.where(col < modes, jnp.stack(parts), jnp.where(col == row + SLOT, 1.0, 0.0))
        pivots = jnp.ones((len(parts), modes, 1), F32)
        for k in range(modes):
            lead = work[:, k : k + 1, :]
            pivot = work[:, k : k + 1, k : k + 1]
            pivots = jnp.where(row[:, :, 0:1] == k, pivot, pivots)
            if k < modes - 1:
                column = jnp.where(row > k, work[:, :, k : k + 1], 0.0)
                work = work - column * (lead * (1.0 / pivot))
        work = work * (float(columns) / jnp.sqrt(pivots))
        for n, s in enumerate(members(i)):
            moved = pltpu.roll(work[n], LANES - SLOT, 1)
            inv_ref[s] = jnp.where(col[0] < modes, moved, 0.0)

    def couple(i):
        parts = spread(finish(packs + i), len(members(i)))
        end = blocks * sections - 1
        for n, s in enumerate(members(i)):
            kept = jnp.where(my_sec * sections + s < end, 1.0 / (columns * math.sqrt(columns)), 0.0)
            coup_ref[s] = parts[n][:, 0:modes] * kept.astype(F32)

    def schedule(events, ready, actions, gap):
        for n, action in enumerate(actions):
            events.setdefault(min(ready + n * gap, sections), []).append(action)

    def run(events, s):
        for at, actions in events.items():
            if at < sections:
                pl.when(s == at)(lambda actions=actions: [action() for action in actions] and None)

    filter_events, apply_events = {}, {}
    for i in range(packs):
        last = members(i)[-1]
        steps = [functools.partial(begin, i), functools.partial(middle, i), functools.partial(factor, i)]
        if last < sections - 1:
            schedule(filter_events, last + 1, steps, 1)
        elif i == 0:
            filter_events.setdefault(sections, []).extend(steps)
        else:
            filter_events.setdefault(sections, []).append(steps[0])
            half = max(1, (i * PER) // 2)
            schedule(apply_events, half, steps[1:2], 0)
            schedule(apply_events, i * PER, steps[2:3], 0)

    def filter_section(s, carry):
        pl.when(s + 2 < sections)(lambda: each_halo(functools.partial(x_copies, s + 2), "send"))
        run(filter_events, s)
        each_halo(functools.partial(x_copies, s), "recv")
        for part, first, rows in ((x_above, 0, WIDTH), (x_own, WIDTH, strip), (x_below, WIDTH + strip, WIDTH)):
            for j in range(groups):
                a_ref[j, first * modes : (first + rows) * modes, :] = part[s, :, j * LANES : (j + 1) * LANES].astype(F32)
        for step in range(STEPS):
            for k in range(DEG):
                src, dst = (a_ref, b_ref) if k % 2 == 0 else (b_ref, a_ref)
                stage(src, dst, k, step * DEG + k + 1, s)
        for r in range(strip):
            for j in range(groups):
                value = a_ref[j, (WIDTH + r) * modes : (WIDTH + r + 1) * modes, :]
                high, low = split_bf16(value)
                split_ref[s, :, (r * groups + j) * LANES : (r * groups + j + 1) * LANES] = jnp.concatenate([high, low], axis=0).astype(BF16)
        gram = dot_nt(split_ref[s], split_ref[s])
        wide_ref[:, 0 : 2 * modes] = gram[0:modes]
        shifted = pltpu.roll(wide_ref[...], LANES - modes, 1)[:, 0:modes]
        wide_ref[...] = jnp.zeros_like(wide_ref)
        place(gram[0:modes, 0:modes] + (shifted + gram[modes : 2 * modes, 0:modes]), s // PER, s)
        return carry

    lax.fori_loop(0, sections, filter_section, 0)
    for action in filter_events.get(sections, []):
        action()

    for i in range(packs):
        last = members(i)[-1]
        steps = [functools.partial(begin, packs + i), functools.partial(middle, packs + i), functools.partial(couple, i)]
        if last < sections - 1:
            schedule(apply_events, last + 2, steps, 1)

    def next_copy():
        return pltpu.make_async_remote_copy(
            src_ref=both_ref.at[0],
            dst_ref=next_ref,
            send_sem=next_send,
            recv_sem=next_recv,
            device_id={"sec": lax.rem(my_sec + blocks - 1, blocks)},
            device_id_type=MESH,
        )

    def apply_section(s, carry):
        run(apply_events, s)
        high, low = split_bf16(inv_ref[s])
        weights = jnp.concatenate([high + pltpu.roll(high, modes, 1), low], axis=0)[:, 0 : 2 * modes].astype(BF16)
        take = max(n for n in range(1, 5) if strip % n == 0)
        for r0 in range(0, strip, take):
            lanes = slice(r0 * columns, (r0 + take) * columns)
            both = dot32(weights, split_ref[s, :, lanes])
            solved = both[0:modes] + both[modes : 2 * modes]
            both_ref[s, :, lanes] = solved.astype(BF16)
            tall = jnp.concatenate([solved[:, r * columns : (r + 1) * columns] for r in range(take)], axis=0)
            stack_ref[r0 * modes : (r0 + take) * modes, :] = tall.astype(BF16)
        wider = max(n for n in range(1, 9) if strip % n == 0) * modes
        for r0 in range(0, strip * modes, wider):
            natural = dot32(stack_ref[r0 : r0 + wider, :], unmix_ref[...])
            for j in range(groups):
                rows_ref[j, r0 : r0 + wider, :] = natural[:, j * LANES : (j + 1) * LANES]
        for m in range(modes):
            for j in range(groups):
                out_buf[s, m, :, j * LANES : (j + 1) * LANES] = rows_ref[j, pl.ds(m, strip, stride=modes), :].astype(BF16)
        store_copy(s).start()

        @pl.when(s > 0)
        def _():
            place(dot_nt(both_ref[s - 1], both_ref[s]), packs + (s - 1) // PER, s - 1)

        if blocks > 1:
            @pl.when((s == 0) & (my_sec > 0))
            def _():
                next_copy().start()

        return carry

    lax.fori_loop(0, sections, apply_section, 0)
    if blocks > 1:
        @pl.when(my_sec < blocks - 1)
        def _():
            next_copy().wait_recv()
            place(dot_nt(both_ref[sections - 1], next_ref[...]), 2 * packs - 1, sections - 1)

    begin(2 * packs - 1)
    for action in apply_events.get(sections, []):
        action()
    middle(2 * packs - 1)
    couple(packs - 1)

    if blocks > 1:
        pl.when(my_sec > 0)(lambda: next_copy().wait_send())
    each_halo(p_copies, "drain")

    def drain(s, carry):
        store_copy(s).wait()
        each_halo(functools.partial(x_copies, s), "drain")
        return carry

    lax.fori_loop(0, sections, drain, 0)
    for i in range(2 * packs):
        for d in range(1, near):
            near_copy(i, d, pos).wait_send()
        for d in range(1, far):
            far_copy(i, d, ring).wait_send()


def per_device(start_modes, permittivity, heights):
    sections, modes, strip, columns = start_modes.shape
    groups = columns // LANES
    packs = -(-sections // PER)
    tiles = lax.axis_size("tile")
    near = inner_size(tiles)
    far = tiles // near
    used = strip + 2 * WIDTH
    hops = len(hops_of(strip))
    height = lax.dynamic_slice_in_dim(heights, lax.axis_index("sec") * sections, sections)[:, None]
    row = lax.axis_index("tile") * strip - WIDTH + jnp.arange(used, dtype=jnp.int32)[None]
    kept_rows = ((row >= 0) & (row < height)).astype(F32).reshape(-1)
    dma = pltpu.SemaphoreType.DMA
    return pl.pallas_call(
        fused_kernel,
        out_shape=[
            jax.ShapeDtypeStruct((sections, modes, strip, columns), BF16),
            jax.ShapeDtypeStruct((sections, modes, modes), F32),
        ],
        in_specs=[
            pl.BlockSpec(memory_space=pltpu.SMEM),
            pl.BlockSpec(memory_space=pl.ANY),
            pl.BlockSpec(memory_space=pltpu.VMEM),
        ],
        out_specs=[pl.BlockSpec(memory_space=pl.ANY), pl.BlockSpec(memory_space=pltpu.VMEM)],
        scratch_shapes=[
            pltpu.VMEM((sections, modes, strip, columns), BF16),
            pltpu.VMEM((sections, strip * modes, columns), BF16),
            pltpu.VMEM((sections, WIDTH * modes, columns), BF16),
            pltpu.VMEM((sections, WIDTH * modes, columns), BF16),
            pltpu.VMEM((strip * sections, columns), BF16),
            pltpu.VMEM((WIDTH * sections, columns), BF16),
            pltpu.VMEM((WIDTH * sections, columns), BF16),
            pltpu.VMEM((groups, used * modes, LANES), F32),
            pltpu.VMEM((groups, used * modes, LANES), F32),
            pltpu.VMEM((DEG, groups, used * sections, LANES), F32),
            pltpu.VMEM((columns, columns), BF16),
            pltpu.VMEM((columns, columns), BF16),
            pltpu.VMEM((sections, 2 * modes, strip * columns), BF16),
            pltpu.VMEM((sections, modes, strip * columns), BF16),
            pltpu.VMEM((modes, strip * columns), BF16),
            pltpu.VMEM((strip * modes, columns), BF16),
            pltpu.VMEM((groups, strip * modes, LANES), F32),
            pltpu.VMEM((sections, modes, strip, columns), BF16),
            pltpu.VMEM((modes, LANES), F32),
            pltpu.VMEM((2 * packs, modes, LANES), F32),
            pltpu.VMEM((2 * packs, near, modes, LANES), F32),
            pltpu.VMEM((2 * packs, far, modes, LANES), F32),
            pltpu.VMEM((2 * packs, modes, LANES), F32),
            pltpu.VMEM((sections, modes, LANES), F32),
            dma((sections,)),
            dma((sections,)),
            dma((2, hops, sections)),
            dma((2, hops, sections)),
            dma((2, hops)),
            dma((2, hops)),
            dma((2 * packs, near)),
            dma((2 * packs, near)),
            dma((2 * packs, far)),
            dma((2 * packs, far)),
            dma,
            dma,
        ],
        compiler_params=pltpu.CompilerParams(collective_id=0, has_side_effects=True, vmem_limit_bytes=60 * 2**20),
        name="fused",
    )(kept_rows, start_modes, permittivity)


def solution(mesh):
    placed = (P("sec", None, "tile", None), P("sec", "tile", None), P())
    return jax.shard_map(
        per_device,
        mesh=mesh,
        in_specs=placed,
        out_specs=(P("sec", None, "tile", None), P("sec", None, None)),
        check_vma=False,
    )
```

```python
import functools
import math

import jax
import jax.numpy as jnp
from jax import lax
from jax.experimental import pallas as pl
from jax.experimental.pallas import tpu as pltpu
from jax.sharding import PartitionSpec as P

STEPS = 3
DEG = 4
SHIFT_DIAG = 3.0
EPS_WEIGHT = 0.25
LOWER_EDGE = 2.0
UPPER_EDGE = 10.75
CENTER = 0.5 * (UPPER_EDGE + LOWER_EDGE)
RADIUS = 0.5 * (UPPER_EDGE - LOWER_EDGE)
WIDTH = STEPS * DEG
LANES = 128
SLOT = 32
CHUNKS = 1
PER = LANES // SLOT

ROOTS = [CENTER + RADIUS * math.cos(math.pi * (2 * k + 1) / (2 * DEG)) for k in (0, 3, 1, 2)]

NT = (((1,), (1,)), ((), ()))
MESH = pl.DeviceIdType.MESH
F32, BF16 = jnp.float32, jnp.bfloat16


def iota(shape, dim):
    return lax.broadcasted_iota(jnp.int32, shape, dim)


def dot32(a, b):
    return jnp.dot(a, b, preferred_element_type=F32)


def dot_nt(a, b):
    return lax.dot_general(a, b, NT, preferred_element_type=F32)


def interleave(columns, groups, inverse=False):
    row, col = iota((columns, columns), 0), iota((columns, columns), 1)
    if inverse:
        row, col = col, row
    return (row == groups * (col % LANES) + col // LANES).astype(BF16)


def inner_size(tiles):
    return max(n for n in range(1, tiles + 1) if tiles % n == 0 and n * n <= tiles)


def split_bf16(value):
    high = value.astype(BF16).astype(F32)
    return high, value - high


def packs_of(sections):
    return -(-(sections - 1) // PER) + 1, -(-sections // PER)


def hops_of(strip):
    plan, done = [], 0
    while done < WIDTH:
        rows = min(strip, WIDTH - done)
        plan.append((len(plan) + 1, rows, done))
        done += rows
    return plan


def fused_kernel(
    heights,
    x_hbm,
    perm_ref,
    out_hbm,
    coup_ref,
    x_buf,
    x_own,
    x_above,
    x_below,
    p_own,
    p_above,
    p_below,
    a_ref,
    b_ref,
    q_ref,
    mix_ref,
    unmix_ref,
    split_ref,
    both_ref,
    next_ref,
    stack_ref,
    rows_ref,
    out_buf,
    wide_ref,
    pack_ref,
    near_ref,
    far_ref,
    mid_ref,
    inv_ref,
    in_sem,
    out_sem,
    halo_send,
    halo_recv,
    perm_send,
    perm_recv,
    near_send,
    near_recv,
    far_send,
    far_recv,
    next_send,
    next_recv,
):
    sections, modes, strip, columns = x_buf.shape
    groups = columns // LANES
    gram_packs, pair_packs = packs_of(sections)
    used = strip + 2 * WIDTH
    tiles, blocks = lax.axis_size("tile"), lax.axis_size("sec")
    me, my_sec = lax.axis_index("tile"), lax.axis_index("sec")
    near = near_ref.shape[1]
    far = far_ref.shape[1]
    pos, ring = lax.rem(me, near), me // near
    top = me * strip - WIDTH
    plan = hops_of(strip)
    mode_tiles = modes // 8

    barrier = pltpu.get_barrier_semaphore()

    def greet(d, carry):
        pl.semaphore_signal(barrier, inc=1, device_id={"tile": lax.rem(me + d, tiles)}, device_id_type=MESH)
        return carry

    lax.fori_loop(1, tiles, greet, 0)
    if blocks > 1:
        pl.semaphore_signal(barrier, inc=1, device_id={"sec": lax.rem(my_sec + 1, blocks)}, device_id_type=MESH)
        pl.semaphore_signal(barrier, inc=1, device_id={"sec": lax.rem(my_sec + blocks - 1, blocks)}, device_id_type=MESH)

    def load_copy(s):
        return pltpu.make_async_copy(x_hbm.at[s], x_buf.at[s], in_sem.at[s])

    def store_copy(s):
        return pltpu.make_async_copy(out_buf.at[s], out_hbm.at[s], out_sem.at[s])

    lax.fori_loop(0, sections, lambda s, c: (load_copy(s).start(), c)[1], 0)

    mix_ref[...] = interleave(columns, groups)
    unmix_ref[...] = interleave(columns, groups, True)
    wide_ref[...] = jnp.zeros_like(wide_ref)
    pack_ref[...] = jnp.zeros_like(pack_ref)

    def blank(ref, unit, lead):
        for hop, rows, done in plan:
            above, below = (WIDTH - done - rows) * unit, done * unit
            zeros = jnp.zeros((rows * unit, columns), BF16)

            @pl.when(me < hop)
            def _():
                ref[0][lead + (slice(above, above + rows * unit),)] = zeros

            @pl.when(me + hop >= tiles)
            def _():
                ref[1][lead + (slice(below, below + rows * unit),)] = zeros

    def halo_copies(own, above, below, send, recv, unit, hop, rows, done, slot, lead):
        h = hop - 1
        down = pltpu.make_async_remote_copy(
            src_ref=own.at[lead + (pl.ds((strip - rows) * unit, rows * unit),)],
            dst_ref=above.at[lead + (pl.ds((WIDTH - done - rows) * unit, rows * unit),)],
            send_sem=send.at[(0, h) + slot],
            recv_sem=recv.at[(0, h) + slot],
            device_id={"tile": lax.rem(me + hop, tiles)},
            device_id_type=MESH,
        )
        up = pltpu.make_async_remote_copy(
            src_ref=own.at[lead + (pl.ds(0, rows * unit),)],
            dst_ref=below.at[lead + (pl.ds(done * unit, rows * unit),)],
            send_sem=send.at[(1, h) + slot],
            recv_sem=recv.at[(1, h) + slot],
            device_id={"tile": lax.rem(me + tiles - hop, tiles)},
            device_id_type=MESH,
        )
        return down, up

    def x_copies(s, hop, rows, done):
        return halo_copies(x_own, x_above, x_below, halo_send, halo_recv, modes, hop, rows, done, (s,), (s,))

    def p_copies(hop, rows, done):
        return halo_copies(p_own, p_above, p_below, perm_send, perm_recv, sections, hop, rows, done, (), ())

    def each_halo(copies, action):
        for hop, rows, done in plan:
            down, up = copies(hop, rows, done)
            if action == "send":
                pl.when(me + hop < tiles)(lambda down=down: down.start())
                pl.when(me >= hop)(lambda up=up: up.start())
            elif action == "recv":
                pl.when(me >= hop)(lambda down=down: down.wait_recv())
                pl.when(me + hop < tiles)(lambda up=up: up.wait_recv())
            else:
                pl.when(me + hop < tiles)(lambda down=down: down.wait_send())
                pl.when(me >= hop)(lambda up=up: up.wait_send())

    def in_use(s, row):
        under = jnp.clip(heights[my_sec * sections + s] - (top + row), 0, 1)
        return (under * jnp.clip(top + row + 1, 0, 1)).astype(F32)

    def prepare(s):
        load_copy(s).wait()
        for m in range(modes):
            for j in range(groups):
                a_ref[j, pl.ds(m, strip, stride=modes), :] = x_buf[s, m, :, j * LANES : (j + 1) * LANES].astype(F32)
        take = max(n for n in range(1, 9) if strip % n == 0) * modes
        for r0 in range(0, strip * modes, take):
            plain = jnp.concatenate(
                [
                    jnp.concatenate([a_ref[j, r0 + r : r0 + r + modes, :] for j in range(groups)], axis=1)
                    * in_use(s, WIDTH + (r0 + r) // modes)
                    for r in range(0, take, modes)
                ],
                axis=0,
            )
            x_own[s, r0 : r0 + take, :] = dot32(plain.astype(BF16), mix_ref[...]).astype(BF16)

    perm = dot32(perm_ref[...].astype(F32).reshape(sections * strip, columns).astype(BF16), mix_ref[...])
    for s in range(sections):
        for j in range(groups):
            b_ref[j, pl.ds(s, strip, stride=sections), :] = perm[s * strip : (s + 1) * strip, j * LANES : (j + 1) * LANES]
    for j in range(groups):
        p_own[:, j * LANES : (j + 1) * LANES] = b_ref[j, 0 : strip * sections, :].astype(BF16)
    prepare(0)
    pl.semaphore_wait(barrier, tiles - 1 + (2 if blocks > 1 else 0))
    each_halo(p_copies, "send")
    each_halo(functools.partial(x_copies, 0), "send")
    blank((p_above, p_below), sections, ())
    blank((x_above, x_below), modes, (0,))

    def prepare_rest(s, carry):
        prepare(s)
        pl.when(s < 1)(lambda: each_halo(functools.partial(x_copies, s), "send"))
        blank((x_above, x_below), modes, (s,))
        return carry

    lax.fori_loop(1, sections, prepare_rest, 0)

    each_halo(p_copies, "recv")
    base = 4.0 + SHIFT_DIAG
    for part, first, rows in ((p_above, 0, WIDTH), (p_own, WIDTH, strip), (p_below, WIDTH + strip, WIDTH)):
        for j in range(groups):
            diag = base - EPS_WEIGHT * part[:, j * LANES : (j + 1) * LANES].astype(F32)
            for i, root in enumerate(ROOTS):
                q_ref[i, j, first * sections : (first + rows) * sections, :] = diag - root

    lane = iota((8, LANES), 1)
    is_first, is_last = lane == 0, lane == LANES - 1

    def tile_at(row, t):
        return pl.ds(pl.multiple_of(row * modes + t * 8, 8), 8)

    def row_of(ref, row):
        return [[ref[j, tile_at(row, t), :] for j in range(groups)] for t in range(mode_tiles)]

    def stage(src, dst, which, order, s):
        count = -(-(used - 2 * order) // CHUNKS)
        low = min(order, used - CHUNKS * count)

        def body(block, carry):
            row0 = low + block * count
            before, here = row_of(src, row0 - 1), row_of(src, row0)
            for i in range(count):
                row = row0 + i
                after = row_of(src, row + 1)
                weight = in_use(s, row)
                q = [jnp.broadcast_to(q_ref[which, j, pl.ds(row * sections + s, 1), :], (8, LANES)) for j in range(groups)]
                for t in range(mode_tiles):
                    h = here[t]
                    left = jnp.where(is_first, 0.0, pltpu.roll(h[groups - 1], 1, 1))
                    right = jnp.where(is_last, 0.0, pltpu.roll(h[0], LANES - 1, 1))
                    for j in range(groups):
                        side = (h[j - 1] if j else left) + (h[j + 1] if j < groups - 1 else right)
                        beside = (before[t][j] + after[t][j]) + side
                        dst[j, tile_at(row, t), :] = q[j] * h[j] - weight * beside
                before, here = here, after
            return carry

        if CHUNKS == 1:
            body(0, 0)
        else:
            lax.fori_loop(0, CHUNKS, body, 0)

    def place(small, target, s):
        wide_ref[:, 0:modes] = small
        moved = pltpu.roll(wide_ref[...], SLOT * lax.rem(s, PER), 1)
        pack_ref[target] = pack_ref[target] + moved

    def near_copy(i, d, slot):
        return pltpu.make_async_remote_copy(
            src_ref=pack_ref.at[i],
            dst_ref=near_ref.at[i, slot],
            send_sem=near_send.at[i, d],
            recv_sem=near_recv.at[i, slot],
            device_id={"tile": ring * near + lax.rem(pos + d, near)},
            device_id_type=MESH,
        )

    def far_copy(i, d, slot):
        return pltpu.make_async_remote_copy(
            src_ref=mid_ref.at[i],
            dst_ref=far_ref.at[i, slot],
            send_sem=far_send.at[i, d],
            recv_sem=far_recv.at[i, slot],
            device_id={"tile": lax.rem(ring + d, far) * near + pos},
            device_id_type=MESH,
        )

    def begin(i):
        for d in range(1, near):
            near_copy(i, d, pos).start()
        near_ref[i, pos] = pack_ref[i]

    def middle(i):
        for d in range(1, near):
            near_copy(i, d, lax.rem(pos + near - d, near)).wait_recv()
        total = near_ref[i, 0]
        for n in range(1, near):
            total = total + near_ref[i, n]
        mid_ref[i] = total
        for d in range(1, far):
            far_copy(i, d, ring).start()
        far_ref[i, ring] = total

    def finish(i):
        for d in range(1, far):
            far_copy(i, d, lax.rem(ring + far - d, far)).wait_recv()
        total = far_ref[i, 0]
        for n in range(1, far):
            total = total + far_ref[i, n]
        return total

    def gram_members(i):
        return range(i * PER, min(sections - 1, (i + 1) * PER)) if i < gram_packs - 1 else range(sections - 1, sections)

    def pair_members(i):
        return range(i * PER, min(sections, (i + 1) * PER))

    def gram_pack(s):
        return s // PER + (s // (sections - 1)) * (gram_packs - 1 - (sections - 1) // PER)

    def spread(total, members):
        return [pltpu.roll(total, (LANES - SLOT * (s % PER)) % LANES, 1) if s % PER else total for s in members]

    def factor(i):
        parts = spread(finish(i), gram_members(i))
        shape = (len(parts), modes, LANES)
        row, col = iota(shape, 1), iota(shape, 2)
        work = jnp.where(col < modes, jnp.stack(parts), jnp.where(col == row + SLOT, 1.0, 0.0))
        pivots = jnp.ones((len(parts), modes, 1), F32)
        for k in range(modes):
            lead = work[:, k : k + 1, :]
            pivot = work[:, k : k + 1, k : k + 1]
            pivots = jnp.where(row[:, :, 0:1] == k, pivot, pivots)
            if k < modes - 1:
                column = jnp.where(row > k, work[:, :, k : k + 1], 0.0)
                work = work - column * (lead * (1.0 / pivot))
        work = work * (float(columns) / jnp.sqrt(pivots))
        for n, s in enumerate(gram_members(i)):
            moved = pltpu.roll(work[n], LANES - SLOT, 1)
            inv_ref[s] = jnp.where(col[0] < modes, moved, 0.0)

    def couple(i):
        parts = spread(finish(gram_packs + i), pair_members(i))
        end = blocks * sections - 1
        for n, s in enumerate(pair_members(i)):
            kept = jnp.where(my_sec * sections + s < end, 1.0 / (columns * math.sqrt(columns)), 0.0)
            coup_ref[s] = parts[n][:, 0:modes] * kept.astype(F32)

    def schedule(events, at, *actions):
        events.setdefault(min(at, sections), []).extend(actions)

    def run(events, s):
        for at, actions in events.items():
            if at < sections:
                pl.when(s == at)(lambda actions=actions: [action() for action in actions] and None)

    filter_events, apply_events = {}, {}
    for i in range(gram_packs):
        first, last = gram_members(i)[0], gram_members(i)[-1]
        steps = [functools.partial(begin, i), functools.partial(middle, i), functools.partial(factor, i)]
        if i == 0:
            for n, step in enumerate(steps):
                schedule(filter_events, last + 1 + n, step)
        else:
            schedule(filter_events, last + 1, steps[0])
            if last + 1 < sections:
                schedule(filter_events, sections, steps[1])
            else:
                schedule(apply_events, max(0, min(PER, last) - 1), steps[1])
            schedule(apply_events, first, steps[2])

    def filter_section(s, carry):
        pl.when(s + 1 < sections)(lambda: each_halo(functools.partial(x_copies, s + 1), "send"))
        run(filter_events, s)
        each_halo(functools.partial(x_copies, s), "recv")
        for part, first, rows in ((x_above, 0, WIDTH), (x_own, WIDTH, strip), (x_below, WIDTH + strip, WIDTH)):
            for j in range(groups):
                a_ref[j, first * modes : (first + rows) * modes, :] = part[s, :, j * LANES : (j + 1) * LANES].astype(F32)
        for step in range(STEPS):
            for k in range(DEG):
                src, dst = (a_ref, b_ref) if k % 2 == 0 else (b_ref, a_ref)
                stage(src, dst, k, step * DEG + k + 1, s)
        for r in range(strip):
            for j in range(groups):
                value = a_ref[j, (WIDTH + r) * modes : (WIDTH + r + 1) * modes, :]
                high, low = split_bf16(value)
                split_ref[s, :, (r * groups + j) * LANES : (r * groups + j + 1) * LANES] = jnp.concatenate([high, low], axis=0).astype(BF16)
        gram = dot_nt(split_ref[s], split_ref[s])
        wide_ref[:, 0 : 2 * modes] = gram[0:modes]
        shifted = pltpu.roll(wide_ref[...], LANES - modes, 1)[:, 0:modes]
        wide_ref[...] = jnp.zeros_like(wide_ref)
        place(gram[0:modes, 0:modes] + (shifted + gram[modes : 2 * modes, 0:modes]), gram_pack(s), s)
        return carry

    lax.fori_loop(0, sections, filter_section, 0)
    for action in filter_events.get(sections, []):
        action()

    for i in range(pair_packs - 1):
        schedule(apply_events, pair_members(i)[-1] + 2, functools.partial(begin, gram_packs + i))

    def next_copy():
        return pltpu.make_async_remote_copy(
            src_ref=both_ref.at[0],
            dst_ref=next_ref,
            send_sem=next_send,
            recv_sem=next_recv,
            device_id={"sec": lax.rem(my_sec + blocks - 1, blocks)},
            device_id_type=MESH,
        )

    def apply_section(s, carry):
        run(apply_events, s)
        high, low = split_bf16(inv_ref[s])
        weights = jnp.concatenate([high + pltpu.roll(high, modes, 1), low], axis=0)[:, 0 : 2 * modes].astype(BF16)
        take = max(n for n in range(1, 5) if strip % n == 0)
        for r0 in range(0, strip, take):
            lanes = slice(r0 * columns, (r0 + take) * columns)
            both = dot32(weights, split_ref[s, :, lanes])
            solved = both[0:modes] + both[modes : 2 * modes]
            both_ref[s, :, lanes] = solved.astype(BF16)
            tall = jnp.concatenate([solved[:, r * columns : (r + 1) * columns] for r in range(take)], axis=0)
            stack_ref[r0 * modes : (r0 + take) * modes, :] = tall.astype(BF16)
        wider = max(n for n in range(1, 9) if strip % n == 0) * modes
        for r0 in range(0, strip * modes, wider):
            natural = dot32(stack_ref[r0 : r0 + wider, :], unmix_ref[...])
            for j in range(groups):
                rows_ref[j, r0 : r0 + wider, :] = natural[:, j * LANES : (j + 1) * LANES]
        for m in range(modes):
            for j in range(groups):
                out_buf[s, m, :, j * LANES : (j + 1) * LANES] = rows_ref[j, pl.ds(m, strip, stride=modes), :].astype(BF16)
        store_copy(s).start()

        @pl.when(s > 0)
        def _():
            place(dot_nt(both_ref[s - 1], both_ref[s]), gram_packs + (s - 1) // PER, s - 1)

        if blocks > 1:
            @pl.when((s == 0) & (my_sec > 0))
            def _():
                next_copy().start()

        return carry

    lax.fori_loop(0, sections, apply_section, 0)
    if blocks > 1:
        @pl.when(my_sec < blocks - 1)
        def _():
            next_copy().wait_recv()
            place(dot_nt(both_ref[sections - 1], next_ref[...]), gram_packs + pair_packs - 1, sections - 1)

    for action in apply_events.get(sections, []):
        action()
    begin(gram_packs + pair_packs - 1)
    for i in range(pair_packs):
        middle(gram_packs + i)
    for i in range(pair_packs):
        couple(i)

    if blocks > 1:
        pl.when(my_sec > 0)(lambda: next_copy().wait_send())
    each_halo(p_copies, "drain")

    def drain(s, carry):
        store_copy(s).wait()
        each_halo(functools.partial(x_copies, s), "drain")
        return carry

    lax.fori_loop(0, sections, drain, 0)
    for i in range(gram_packs + pair_packs):
        for d in range(1, near):
            near_copy(i, d, pos).wait_send()
        for d in range(1, far):
            far_copy(i, d, ring).wait_send()


def per_device(start_modes, permittivity, heights):
    sections, modes, strip, columns = start_modes.shape
    groups = columns // LANES
    packs = sum(packs_of(sections))
    tiles = lax.axis_size("tile")
    near = inner_size(tiles)
    far = tiles // near
    used = strip + 2 * WIDTH
    hops = len(hops_of(strip))
    dma = pltpu.SemaphoreType.DMA
    return pl.pallas_call(
        fused_kernel,
        out_shape=[
            jax.ShapeDtypeStruct((sections, modes, strip, columns), BF16),
            jax.ShapeDtypeStruct((sections, modes, modes), F32),
        ],
        in_specs=[
            pl.BlockSpec(memory_space=pltpu.SMEM),
            pl.BlockSpec(memory_space=pl.ANY),
            pl.BlockSpec(memory_space=pltpu.VMEM),
        ],
        out_specs=[pl.BlockSpec(memory_space=pl.ANY), pl.BlockSpec(memory_space=pltpu.VMEM)],
        scratch_shapes=[
            pltpu.VMEM((sections, modes, strip, columns), BF16),
            pltpu.VMEM((sections, strip * modes, columns), BF16),
            pltpu.VMEM((sections, WIDTH * modes, columns), BF16),
            pltpu.VMEM((sections, WIDTH * modes, columns), BF16),
            pltpu.VMEM((strip * sections, columns), BF16),
            pltpu.VMEM((WIDTH * sections, columns), BF16),
            pltpu.VMEM((WIDTH * sections, columns), BF16),
            pltpu.VMEM((groups, used * modes, LANES), F32),
            pltpu.VMEM((groups, used * modes, LANES), F32),
            pltpu.VMEM((DEG, groups, used * sections, LANES), F32),
            pltpu.VMEM((columns, columns), BF16),
            pltpu.VMEM((columns, columns), BF16),
            pltpu.VMEM((sections, 2 * modes, strip * columns), BF16),
            pltpu.VMEM((sections, modes, strip * columns), BF16),
            pltpu.VMEM((modes, strip * columns), BF16),
            pltpu.VMEM((strip * modes, columns), BF16),
            pltpu.VMEM((groups, strip * modes, LANES), F32),
            pltpu.VMEM((sections, modes, strip, columns), BF16),
            pltpu.VMEM((modes, LANES), F32),
            pltpu.VMEM((packs, modes, LANES), F32),
            pltpu.VMEM((packs, near, modes, LANES), F32),
            pltpu.VMEM((packs, far, modes, LANES), F32),
            pltpu.VMEM((packs, modes, LANES), F32),
            pltpu.VMEM((sections, modes, LANES), F32),
            dma((sections,)),
            dma((sections,)),
            dma((2, hops, sections)),
            dma((2, hops, sections)),
            dma((2, hops)),
            dma((2, hops)),
            dma((packs, near)),
            dma((packs, near)),
            dma((packs, far)),
            dma((packs, far)),
            dma,
            dma,
        ],
        compiler_params=pltpu.CompilerParams(collective_id=0, has_side_effects=True, vmem_limit_bytes=60 * 2**20),
        name="fused",
    )(heights, start_modes, permittivity)


def solution(mesh):
    placed = (P("sec", None, "tile", None), P("sec", "tile", None), P())
    return jax.shard_map(
        per_device,
        mesh=mesh,
        in_specs=placed,
        out_specs=(P("sec", None, "tile", None), P("sec", None, None)),
        check_vma=False,
    )
```
